32 devices in a mesh: section: 4 (over x, core), row: 4 (over z), col: 2 (over y).
Axes of the slice: x: 2, y: 2, z: 4, core: 2. Of those that a mesh axis runs over, the one named last changes fastest.
Arguments:
- frames: bfloat16 [3, 64, 64, 128], P(None, 'row', 'col'), may hold values from -6 to 6
- gate_weight: bfloat16 [4, 9, 256, 512], P('section'), may hold values from -0.16666667 to 0.16666667
- gate_bias: float32 [4, 512], P('section'), may hold values from -4 to 4
Outputs:
- hidden_final: bfloat16 [4, 64, 64, 128], P('section', 'row', 'col')
- cell_final: float32 [4, 64, 64, 128], P('section', 'row', 'col')
The draws below stay inside these ranges and needn't reach their ends.
All inputs are finite; a program needn't handle non-finite values.
Results may differ from the reference program's by a relative error of at most 0.0033.
Values may be sent and summed in bfloat16 or wider, within the bound.
A program may use at most 64 MiB of HBM per device.

```python
import jax
import jax.numpy as jnp

HID = 128
FRAMES = 3
LAYERS = 4
NR = 64
NC = 64


def draw_frames(key, part):
    whole_shape = (FRAMES, NR, NC, HID)
    grid_rows = jnp.arange(NR)[:, None]
    grid_cols = jnp.arange(NC)[None, :]
    checker = 1.0 - 2.0 * ((grid_rows + grid_cols) % 2).astype(jnp.float32)
    magnitude = jnp.minimum(jnp.abs(jax.random.normal(key, whole_shape, jnp.float32)), 6.0)
    return (magnitude * checker[None, :, :, None]).astype(jnp.bfloat16)


def draw_gate_weight(key, part):
    whole_shape = (LAYERS, 9, 2 * HID, 4 * HID)
    base_scale = (18.0 * HID) ** (-0.5)
    factors = jnp.array([4.0, 1.0, 4.0, 1.0, 0.5, 1.0, 4.0, 1.0, 4.0], jnp.float32) * base_scale
    values = jax.random.normal(key, whole_shape, jnp.float32)
    scaled = values * factors[None, :, None, None]
    limit = 7.96 * base_scale
    return jnp.clip(scaled, -limit, limit).astype(jnp.bfloat16)


def levels(stream_key, dims, cuts, least, largest):
    loudness = 1.0
    for dim, blocks in cuts:
        heights = jax.random.uniform(jax.random.fold_in(jax.random.fold_in(stream_key, 6), dim), (blocks,), jnp.float32, least / len(cuts), largest / len(cuts))
        loudness = loudness * jnp.repeat(jnp.exp(heights), dims[dim] // blocks).reshape((-1,) + (1,) * (len(dims) - 1 - dim))
    return loudness


def gaussian(rng, dims, spread, reach, shards=(), dtype=jnp.bfloat16):
    values = jax.random.normal(rng, dims, jnp.float32) * spread
    if len(shards) > 0:
        values = levels(rng, dims, shards, -0.22, 0.18) * values
    return jnp.clip(values, min=-reach, max=reach).astype(dtype)


def setup_inputs(seed: int = 0) -> dict:
    arg_keys = jax.random.split(jax.random.key(seed), 4)
    frames = draw_frames(jax.random.fold_in(arg_keys[3], 71), 0)
    gate_weight = draw_gate_weight(jax.random.fold_in(arg_keys[3], 71), 0)
    gate_bias = gaussian(arg_keys[2], (LAYERS, 4 * HID), 1.0, 4.0, ((0, 4),), jnp.float32)
    return dict(frames=frames, gate_weight=gate_weight, gate_bias=gate_bias)


def convolve(stack, kernel, bias):
    rows, cols = stack.shape[0], stack.shape[1]
    padded = jnp.pad(stack, ((1, 1), (1, 1), (0, 0)))
    total = jnp.zeros((rows * cols, kernel.shape[-1]), jnp.float32) + bias
    for offset in range(9):
        drow, dcol = offset // 3, offset % 3
        window = padded[drow:drow + rows, dcol:dcol + cols].reshape(rows * cols, -1)
        total = total + jnp.dot(window, kernel[offset], preferred_element_type=jnp.float32)
    return total.reshape(rows, cols, -1)


def reference(frames, gate_weight, gate_bias):
    nlayer = gate_weight.shape[0]
    width = frames.shape[-1]
    inputs = [frames[t] for t in range(frames.shape[0])]
    hiddens = []
    cells = []
    for layer in range(nlayer):
        hidden = jnp.zeros(frames.shape[1:], jnp.bfloat16)
        cell = jnp.zeros(frames.shape[1:], jnp.float32)
        outputs = []
        for t in range(len(inputs)):
            stack = jnp.concatenate([inputs[t], hidden], axis=-1)
            pre = convolve(stack, gate_weight[layer], gate_bias[layer])
            gate_in = pre[..., :width]
            forget = pre[..., width:2 * width]
            candidate = pre[..., 2 * width:3 * width]
            gate_out = pre[..., 3 * width:]
            cell = jax.nn.sigmoid(forget) * cell + jax.nn.sigmoid(gate_in) * jnp.tanh(candidate)
            hidden = (jax.nn.sigmoid(gate_out) * jnp.tanh(cell)).astype(jnp.bfloat16)
            outputs.append(hidden)
        inputs = outputs
        hiddens.append(hidden)
        cells.append(cell)
    return jnp.stack(hiddens), jnp.stack(cells)
```

```python
import jax
import jax.numpy as jnp
from jax import lax
from jax.experimental import pallas as pl
from jax.experimental.pallas import tpu as pltpu
from jax.sharding import PartitionSpec as P

MESH = pl.DeviceIdType.MESH
DIRS = [(dr, dc) for dr in (-1, 0, 1) for dc in (-1, 0, 1) if (dr, dc) != (0, 0)]
CHUNK = 4


def sigmoid(v):
    return 0.5 * jnp.tanh(0.5 * v) + 0.5


def slot(dr, dc):
    return (dr + 1) * 3 + (dc + 1)


def body(sizes, frames, weight, bias, hid_out, cell_out,
         xc, xe, hc, he, col_x, col_h, w, ax, ah, acc,
         local_sem, send_sem, xrecv, hrecv):
    nsec, nrow, ncol = sizes
    steps, rows, cols, width = frames.shape
    sec, row, col = lax.axis_index("section"), lax.axis_index("row"), lax.axis_index("col")

    def load_frame(t):
        return pltpu.make_async_copy(frames.at[t], xc.at[t, pl.ds(1, rows)], local_sem.at[t])

    load_w = pltpu.make_async_copy(weight.at[0], w, local_sem.at[steps])

    @pl.when(sec == 0)
    def _():
        for t in range(steps):
            load_frame(t).start()

    load_w.start()

    def there(dr, dc):
        ok = sec >= 0
        if dr:
            ok = (row > 0) if dr < 0 else (row < nrow - 1)
        if dc:
            okc = (col > 0) if dc < 0 else (col < ncol - 1)
            ok = jnp.logical_and(ok, okc) if dr else okc
        return ok

    def device(ds, dr, dc):
        return {"section": sec + ds, "row": row + dr, "col": col + dc}

    zrow = jnp.zeros((cols, width), jnp.bfloat16)
    for buf, edge in ((xc, xe), (hc, he)):
        for t in range(edge.shape[0]):
            buf[t, 0] = zrow
            buf[t, rows + 1] = zrow
            edge[t] = jnp.zeros(edge.shape[1:], jnp.bfloat16)

    barrier = pltpu.get_barrier_semaphore()
    for ds in (-1, 0, 1):
        okd = (sec > 0) if ds < 0 else (sec < nsec - 1)
        if ds:
            @pl.when(okd)
            def _(ds=ds):
                pl.semaphore_signal(barrier, inc=1, device_id=device(ds, 0, 0), device_id_type=MESH)
        for dr, dc in DIRS:
            ok = there(dr, dc)
            if ds:
                ok = jnp.logical_and(ok, okd)

            @pl.when(ok)
            def _(ds=ds, dr=dr, dc=dc):
                pl.semaphore_signal(barrier, inc=1, device_id=device(ds, dr, dc), device_id_type=MESH)

    def extent(pos, count):
        return 1 + jnp.where(pos > 0, 1, 0) + jnp.where(pos < count - 1, 1, 0)

    pl.semaphore_wait(barrier, extent(sec, nsec) * extent(row, nrow) * extent(col, ncol) - 1)

    def halo_copy(center, colbuf, t, kind, ds, dr, dc, to_c, to_e, recv):
        if dc == 0:
            src = center.at[t, rows if dr > 0 else 1]
            dst = to_c.at[t, 0 if dr > 0 else rows + 1]
        else:
            src = colbuf.at[t, 1 if dc > 0 else 0]
            dst = to_e.at[t, (0 if dc > 0 else 3) + (1 - dr)]
        return pltpu.make_async_remote_copy(
            src_ref=src, dst_ref=dst,
            send_sem=send_sem.at[t, kind, slot(dr, dc)],
            recv_sem=recv.at[t, slot(-dr, -dc)],
            device_id=device(ds, dr, dc), device_id_type=MESH,
        )

    def halo_sends(act, center, colbuf, t, kind, ds, to_c, to_e, recv):
        for dr, dc in DIRS:
            @pl.when(there(dr, dc))
            def _(dr=dr, dc=dc):
                copy = halo_copy(center, colbuf, t, kind, ds, dr, dc, to_c, to_e, recv)
                copy.start() if act == "start" else copy.wait_send()

    def halo_waits(t, to_c, to_e, recv):
        for dr, dc in DIRS:
            @pl.when(there(dr, dc))
            def _(dr=dr, dc=dc):
                if dc == 0:
                    dst = to_c.at[t, 0 if dr < 0 else rows + 1]
                else:
                    dst = to_e.at[t, (0 if dc < 0 else 3) + (1 + dr)]
                pltpu.make_async_remote_copy(
                    src_ref=dst, dst_ref=dst,
                    send_sem=send_sem.at[t, 0, slot(0, 0)],
                    recv_sem=recv.at[t, slot(dr, dc)],
                    device_id=device(0, dr, dc), device_id_type=MESH,
                ).wait_recv()

    def center_copy(t):
        return pltpu.make_async_remote_copy(
            src_ref=hc.at[t, pl.ds(1, rows)], dst_ref=xc.at[t, pl.ds(1, rows)],
            send_sem=send_sem.at[t, 1, slot(0, 0)], recv_sem=xrecv.at[t, slot(0, 0)],
            device_id=device(1, 0, 0), device_id_type=MESH,
        )

    def stage_columns(center, t, colbuf):
        value = center[t, pl.ds(1, rows)].astype(jnp.float32)
        colbuf[t, 0] = value[:, 0, :].astype(jnp.bfloat16)
        colbuf[t, 1] = value[:, cols - 1, :].astype(jnp.bfloat16)

    @pl.when(sec == 0)
    def _():
        for t in range(steps):
            load_frame(t).wait()
            stage_columns(xc, t, col_x)
            halo_sends("start", xc, col_x, t, 2, 0, xc, xe, xrecv)

    place = lax.broadcasted_iota(jnp.int32, (cols, width), 0)

    def assemble(center, edge, t, out):
        ends = [edge[t, k].astype(jnp.float32) for k in range(6)]
        for r in range(rows + 2):
            line = center[t, r]
            wide = line.astype(jnp.float32)
            halos = []
            for side in (0, 3):
                if r == 0:
                    halos.append(ends[side][rows - 1:rows])
                elif r == rows + 1:
                    halos.append(ends[side + 2][0:1])
                else:
                    halos.append(ends[side + 1][r - 1:r])
            before = jnp.where(place == 0, halos[0], pltpu.roll(wide, 1, 0))
            after = jnp.where(place == cols - 1, halos[1], pltpu.roll(wide, cols - 1, 0))
            out[r, :, 0:width] = before.astype(jnp.bfloat16)
            out[r, :, width:2 * width] = line
            out[r, :, 2 * width:3 * width] = after.astype(jnp.bfloat16)

    def patches(a, first, count):
        return jnp.concatenate(
            [a[first + k:first + k + count].reshape(count * cols, 3 * width) for k in range(3)], axis=-1
        )

    def kernel_of(half):
        return w[:, half * width:(half + 1) * width, :].reshape(9 * width, 4 * width)

    for t in range(steps):
        if t > 0:
            halo_waits(t - 1, hc, he, hrecv)
            assemble(hc, he, t - 1, ah)
            acc[...] = jnp.dot(patches(ah, 0, rows), kernel_of(1), preferred_element_type=jnp.float32)

        @pl.when(sec > 0)
        def _(t=t):
            center = xc.at[t, pl.ds(1, rows)]
            pltpu.make_async_remote_copy(
                src_ref=center, dst_ref=center, send_sem=send_sem.at[t, 0, slot(0, 0)],
                recv_sem=xrecv.at[t, slot(0, 0)], device_id=device(-1, 0, 0), device_id_type=MESH,
            ).wait_recv()

        halo_waits(t, xc, xe, xrecv)
        assemble(xc, xe, t, ax)
        if t == 0:
            load_w.wait()
        for r in range(0, rows, CHUNK):
            part = pl.ds(r * cols, CHUNK * cols)
            pre = jnp.dot(patches(ax, r, CHUNK), kernel_of(0), preferred_element_type=jnp.float32)
            pre = pre + bias[...]
            if t > 0:
                pre = pre + acc[part]
            gate_in = sigmoid(pre[:, :width])
            cand = jnp.tanh(pre[:, 2 * width:3 * width])
            cell = gate_in * cand
            area = pl.ds(r, CHUNK)
            if t > 0:
                old = cell_out[0, area].reshape(CHUNK * cols, width)
                cell = sigmoid(pre[:, width:2 * width]) * old + cell
            hidden = sigmoid(pre[:, 3 * width:]) * jnp.tanh(cell)
            cell_out[0, area] = cell.reshape(CHUNK, cols, width)
            hidden = hidden.astype(jnp.bfloat16).reshape(CHUNK, cols, width)
            hc[t, pl.ds(r + 1, CHUNK)] = hidden
            if t == steps - 1:
                hid_out[0, area] = hidden
        stage_columns(hc, t, col_h)

        @pl.when(sec < nsec - 1)
        def _(t=t):
            center_copy(t).start()
            halo_sends("start", hc, col_h, t, 1, 1, xc, xe, xrecv)

        if t < steps - 1:
            halo_sends("start", hc, col_h, t, 0, 0, hc, he, hrecv)

    @pl.when(sec == 0)
    def _():
        for t in range(steps):
            halo_sends("wait", xc, col_x, t, 2, 0, xc, xe, xrecv)

    @pl.when(sec < nsec - 1)
    def _():
        for t in range(steps):
            center_copy(t).wait_send()
            halo_sends("wait", hc, col_h, t, 1, 1, xc, xe, xrecv)

    for t in range(steps - 1):
        halo_sends("wait", hc, col_h, t, 0, 0, hc, he, hrecv)


def solution(mesh):
    sizes = (mesh.shape["section"], mesh.shape["row"], mesh.shape["col"])

    def step(frames, weight, bias):
        steps, rows, cols, width = frames.shape
        vmem = pl.BlockSpec(memory_space=pltpu.VMEM)
        hbm = pl.BlockSpec(memory_space=pl.ANY)
        bf16 = jnp.bfloat16
        return pl.pallas_call(
            lambda *refs: body(sizes, *refs),
            out_shape=(
                jax.ShapeDtypeStruct((1, rows, cols, width), bf16),
                jax.ShapeDtypeStruct((1, rows, cols, width), jnp.float32),
            ),
            in_specs=[hbm, hbm, vmem],
            out_specs=(vmem, vmem),
            scratch_shapes=[
                pltpu.VMEM((steps, rows + 2, cols, width), bf16),
                pltpu.VMEM((steps, 6, rows, width), bf16),
                pltpu.VMEM((steps, rows + 2, cols, width), bf16),
                pltpu.VMEM((steps, 6, rows, width), bf16),
                pltpu.VMEM((steps, 2, rows, width), bf16),
                pltpu.VMEM((steps, 2, rows, width), bf16),
                pltpu.VMEM(weight.shape[1:], bf16),
                pltpu.VMEM((rows + 2, cols, 3 * width), bf16),
                pltpu.VMEM((rows + 2, cols, 3 * width), bf16),
                pltpu.VMEM((rows * cols, 4 * width), jnp.float32),
                pltpu.SemaphoreType.DMA((steps + 1,)),
                pltpu.SemaphoreType.DMA((steps, 3, 9)),
                pltpu.SemaphoreType.DMA((steps, 9)),
                pltpu.SemaphoreType.DMA((steps, 9)),
            ],
            compiler_params=pltpu.CompilerParams(collective_id=0, has_side_effects=True),
        )(frames, weight, bias)

    return jax.shard_map(
        step,
        mesh=mesh,
        in_specs=(P(None, "row", "col", None), P("section", None, None, None), P("section", None)),
        out_specs=(P("section", "row", "col", None), P("section", "row", "col", None)),
        check_vma=False,
    )
```

```python
import jax
import jax.numpy as jnp
from jax import lax
from jax.experimental import pallas as pl
from jax.experimental.pallas import tpu as pltpu
from jax.sharding import PartitionSpec as P

MESH = pl.DeviceIdType.MESH
DIRS = [(dr, dc) for dr in (-1, 0, 1) for dc in (-1, 0, 1) if (dr, dc) != (0, 0)]
PAD = 8
CHUNK = 8


def sigmoid(v):
    return 0.5 * jnp.tanh(0.5 * v) + 0.5


def slot(dr, dc):
    return (dr + 1) * 3 + (dc + 1)


def body(sizes, frames, weight, bias, hid_out, cell_out,
         xc, xe, fe, hc, he, col_x, col_h, w, ax, ah, acc, cell_mem,
         local_sem, send_sem, frecv, xrecv, hrecv):
    nsec, nrow, ncol = sizes
    steps, rows, cols, width = frames.shape
    high = rows + 2 * PAD
    sec, row, col = lax.axis_index("section"), lax.axis_index("row"), lax.axis_index("col")

    def load_frame(t):
        return pltpu.make_async_copy(frames.at[t], xc.at[t, pl.ds(PAD, rows)], local_sem.at[t])

    load_w = pltpu.make_async_copy(weight.at[0], w, local_sem.at[steps])

    @pl.when(sec == 0)
    def _():
        for t in range(steps):
            load_frame(t).start()

    load_w.start()

    def there(dr, dc):
        ok = sec >= 0
        if dr:
            ok = (row > 0) if dr < 0 else (row < nrow - 1)
        if dc:
            okc = (col > 0) if dc < 0 else (col < ncol - 1)
            ok = jnp.logical_and(ok, okc) if dr else okc
        return ok

    def device(ds, dr, dc):
        return {"section": sec + ds, "row": row + dr, "col": col + dc}

    @pl.when(sec == 0)
    def _():
        for t in range(steps):
            fe[t] = jnp.zeros(fe.shape[1:], jnp.bfloat16)
            xc[t, 0:PAD] = jnp.zeros((PAD, cols, width), jnp.bfloat16)
            xc[t, PAD + rows:high] = jnp.zeros((PAD, cols, width), jnp.bfloat16)

    for t in range(steps):
        xe[t] = jnp.zeros(xe.shape[1:], jnp.bfloat16)
        he[t] = jnp.zeros(he.shape[1:], jnp.bfloat16)

    barrier = pltpu.get_barrier_semaphore()
    for ds in (-1, 0, 1):
        okd = (sec > 0) if ds < 0 else (sec < nsec - 1) if ds > 0 else (sec == 0)
        for dr, dc in [(0, 0)] + DIRS:
            if (ds == 0 and (dr, dc) == (0, 0)) or (ds and dr):
                continue
            ok = there(dr, dc)
            if ds or dr:
                ok = jnp.logical_and(ok, okd)

            @pl.when(ok)
            def _(ds=ds, dr=dr, dc=dc):
                pl.semaphore_signal(barrier, inc=1, device_id=device(ds, dr, dc), device_id_type=MESH)

    def extent(pos, count):
        return 1 + jnp.where(pos > 0, 1, 0) + jnp.where(pos < count - 1, 1, 0)

    wide_cols = extent(col, ncol)
    extra = jnp.where(sec == 0, (extent(row, nrow) - 1) * wide_cols, 0)
    pl.semaphore_wait(barrier, extent(sec, nsec) * wide_cols - 1 + extra)

    top = jnp.where(row > 0, 1.0, 0.0)
    bottom = jnp.where(row < nrow - 1, 1.0, 0.0)
    place = lax.broadcasted_iota(jnp.int32, (cols, width), 0)

    def remote(src, dst, send, recv, ds, dr, dc):
        return pltpu.make_async_remote_copy(
            src_ref=src, dst_ref=dst, send_sem=send, recv_sem=recv,
            device_id=device(ds, dr, dc), device_id_type=MESH,
        )

    def stage_columns(value, store):
        value = value.astype(jnp.float32)
        store[0] = value[:, 0, :].astype(jnp.bfloat16)
        store[1] = value[:, cols - 1, :].astype(jnp.bfloat16)

    def assemble(center, ends, t, first, last, out):
        for r in range(first, last):
            line = center[t, r]
            wide = line.astype(jnp.float32)
            before = jnp.where(place == 0, ends[0][r:r + 1], pltpu.roll(wide, 1, 0))
            after = jnp.where(place == cols - 1, ends[1][r:r + 1], pltpu.roll(wide, cols - 1, 0))
            out[r, :, 0:width] = before.astype(jnp.bfloat16)
            out[r, :, width:2 * width] = line
            out[r, :, 2 * width:3 * width] = after.astype(jnp.bfloat16)

    def patches(a, first, count):
        return jnp.concatenate(
            [a[first + k:first + k + count].reshape(count * cols, 3 * width) for k in (-1, 0, 1)], axis=-1
        )

    def kernel_of(half):
        return w[:, half * width:(half + 1) * width, :].reshape(9 * width, 4 * width)

    def column_copy(t, kind, ds, dc, to, recv):
        side = 1 if dc > 0 else 0
        return remote(col_h.at[t, side], to.at[t, 1 - side], send_sem.at[t, kind, side],
                      recv.at[t, 1 - side], ds, 0, dc)

    def pieces(first, last):
        return [(r, min(CHUNK, last - r)) for r in range(first, last, CHUNK)]

    def block_copy(t, n, r, count, ds):
        part = pl.ds(r, count)
        return remote(hc.at[t, part], xc.at[t, part], send_sem.at[t, 1, 2 + n], xrecv.at[t, 2 + n], ds, 0, 0)

    def frame_copy(t, reach, dr, dc):
        if dc == 0:
            src = frames.at[t, pl.ds(0 if dr < 0 else rows - reach, reach)]
            dst = xc.at[t, pl.ds(PAD + rows if dr < 0 else PAD - reach, reach)]
        else:
            src = col_x.at[t, 1 if dc > 0 else 0]
            dst = fe.at[t, (0 if dc > 0 else 3) + (1 - dr)]
        return remote(src, dst, send_sem.at[t, 2, slot(dr, dc)], frecv.at[t, slot(-dr, -dc)], 0, dr, dc)

    def frame_wait(t, reach, dr, dc):
        if dc == 0:
            dst = xc.at[t, pl.ds(PAD - reach if dr < 0 else PAD + rows, reach)]
        else:
            dst = fe.at[t, (0 if dc < 0 else 3) + (1 + dr)]
        remote(dst, dst, send_sem.at[t, 0, 0], frecv.at[t, slot(dr, dc)], 0, dr, dc).wait_recv()

    def section(s):
        def spread(at, t):
            return (nsec - 1 - at) + (steps - 1 - t)

        def columns(act, t, kind, ds, to, recv):
            for dc in (-1, 1):
                @pl.when(there(0, dc))
                def _(dc=dc):
                    copy = column_copy(t, kind, ds, dc, to, recv)
                    copy.start() if act == "start" else copy.wait_send()

        def column_waits(t, to, recv):
            for dc in (-1, 1):
                @pl.when(there(0, dc))
                def _(dc=dc):
                    side = 0 if dc < 0 else 1
                    remote(to.at[t, side], to.at[t, side], send_sem.at[t, 0, side],
                           recv.at[t, side], 0, 0, dc).wait_recv()

        def frame_sends(act):
            for t in range(steps):
                for dr, dc in DIRS:
                    @pl.when(there(dr, dc))
                    def _(t=t, dr=dr, dc=dc):
                        copy = frame_copy(t, spread(0, t) + 1, dr, dc)
                        copy.start() if act == "start" else copy.wait_send()

        if s == 0:
            for t in range(steps):
                load_frame(t).wait()
                stage_columns(xc[t, PAD:PAD + rows], col_x.at[t])
            frame_sends("start")

        for t in range(steps):
            e = spread(s, t)
            first, last = PAD - e, PAD + rows + e
            if t > 0:
                column_waits(t - 1, he, hrecv)
                ends = [he[t - 1, k].astype(jnp.float32) for k in range(2)]
                assemble(hc, ends, t - 1, first - 1, last + 1, ah)
                span = pl.ds(first * cols, (last - first) * cols)
                acc[span] = jnp.dot(patches(ah, first, last - first), kernel_of(1),
                                    preferred_element_type=jnp.float32)
            if s == 0:
                for dr, dc in DIRS:
                    @pl.when(there(dr, dc))
                    def _(dr=dr, dc=dc):
                        frame_wait(t, e + 1, dr, dc)
                ends = [
                    jnp.concatenate([
                        fe[t, k].astype(jnp.float32)[rows - PAD:],
                        fe[t, k + 1].astype(jnp.float32),
                        fe[t, k + 2].astype(jnp.float32)[:PAD],
                    ], axis=0)
                    for k in (0, 3)
                ]
            else:
                for n, (r, count) in enumerate(pieces(first - 1, last + 1)):
                    block_copy(t, n, r, count, -1).wait_recv()
                column_waits(t, xe, xrecv)
                ends = [xe[t, k].astype(jnp.float32) for k in range(2)]
            assemble(xc, ends, t, first - 1, last + 1, ax)
            if t == 0:
                load_w.wait()
            for n, (r, count) in enumerate(pieces(first, last)):
                part = pl.ds(r * cols, count * cols)
                pre = jnp.dot(patches(ax, r, count), kernel_of(0), preferred_element_type=jnp.float32)
                pre = pre + bias[...]
                if t > 0:
                    pre = pre + acc[part]
                cell = sigmoid(pre[:, :width]) * jnp.tanh(pre[:, 2 * width:3 * width])
                if t > 0:
                    cell = sigmoid(pre[:, width:2 * width]) * cell_mem[part] + cell
                hidden = sigmoid(pre[:, 3 * width:]) * jnp.tanh(cell)
                hidden = hidden.reshape(count, cols, width)
                above, below = max(0, PAD - r), max(0, r + count - PAD - rows)
                if above or below:
                    bands = [hidden[:above] * top, hidden[above:count - below], hidden[count - below:] * bottom]
                    hidden = jnp.concatenate([b for b in bands if b.shape[0]], axis=0)
                hidden = hidden.astype(jnp.bfloat16)
                if t < steps - 1:
                    cell_mem[part] = cell
                    hc[t, pl.ds(r, count)] = hidden
                else:
                    if s < nsec - 1:
                        hc[t, pl.ds(r, count)] = hidden
                    low, up = max(r, PAD), min(r + count, PAD + rows)
                    if low < up:
                        cell_out[0, low - PAD:up - PAD] = cell.reshape(count, cols, width)[low - r:up - r]
                        hid_out[0, low - PAD:up - PAD] = hidden[low - r:up - r]
                if s < nsec - 1:
                    block_copy(t, n, r, count, 1).start()
            if t < steps - 1 or s < nsec - 1:
                stage_columns(hc[t], col_h.at[t])
            if t < steps - 1:
                columns("start", t, 0, 0, he, hrecv)
            if s < nsec - 1:
                columns("start", t, 1, 1, xe, xrecv)

        if s == 0:
            frame_sends("wait")
        for t in range(steps):
            if t < steps - 1:
                columns("wait", t, 0, 0, he, hrecv)
            if s < nsec - 1:
                columns("wait", t, 1, 1, xe, xrecv)
                e = spread(s, t)
                for n, (r, count) in enumerate(pieces(PAD - e, PAD + rows + e)):
                    block_copy(t, n, r, count, 1).wait_send()

    for s in range(nsec):
        @pl.when(sec == s)
        def _(s=s):
            section(s)


def solution(mesh):
    sizes = (mesh.shape["section"], mesh.shape["row"], mesh.shape["col"])

    def step(frames, weight, bias):
        steps, rows, cols, width = frames.shape
        high = rows + 2 * PAD
        vmem = pl.BlockSpec(memory_space=pltpu.VMEM)
        hbm = pl.BlockSpec(memory_space=pl.ANY)
        bf16 = jnp.bfloat16
        return pl.pallas_call(
            lambda *refs: body(sizes, *refs),
            out_shape=(
                jax.ShapeDtypeStruct((1, rows, cols, width), bf16),
                jax.ShapeDtypeStruct((1, rows, cols, width), jnp.float32),
            ),
            in_specs=[hbm, hbm, vmem],
            out_specs=(vmem, vmem),
            scratch_shapes=[
                pltpu.VMEM((steps, high, cols, width), bf16),
                pltpu.VMEM((steps, 2, high, width), bf16),
                pltpu.VMEM((steps, 6, rows, width), bf16),
                pltpu.VMEM((steps, high, cols, width), bf16),
                pltpu.VMEM((steps, 2, high, width), bf16),
                pltpu.VMEM((steps, 2, rows, width), bf16),
                pltpu.VMEM((steps, 2, high, width), bf16),
                pltpu.VMEM(weight.shape[1:], bf16),
                pltpu.VMEM((high, cols, 3 * width), bf16),
                pltpu.VMEM((high, cols, 3 * width), bf16),
                pltpu.VMEM((high * cols, 4 * width), jnp.float32),
                pltpu.VMEM((high * cols, width), jnp.float32),
                pltpu.SemaphoreType.DMA((steps + 1,)),
                pltpu.SemaphoreType.DMA((steps, 3, 9)),
                pltpu.SemaphoreType.DMA((steps, 9)),
                pltpu.SemaphoreType.DMA((steps, 9)),
                pltpu.SemaphoreType.DMA((steps, 2)),
            ],
            compiler_params=pltpu.CompilerParams(collective_id=0, has_side_effects=True),
        )(frames, weight, bias)

    return jax.shard_map(
        step,
        mesh=mesh,
        in_specs=(P(None, "row", "col", None), P("section", None, None, None), P("section", None)),
        out_specs=(P("section", "row", "col", None), P("section", "row", "col", None)),
        check_vma=False,
    )
```

```python
import jax
import jax.numpy as jnp
from jax import lax
from jax.experimental import pallas as pl
from jax.experimental.pallas import tpu as pltpu
from jax.sharding import PartitionSpec as P

MESH = pl.DeviceIdType.MESH
DIRS = [(dr, dc) for dr in (-1, 0, 1) for dc in (-1, 0, 1) if (dr, dc) != (0, 0)]
SIDE = 8
CHUNK = 6


def sigmoid(v):
    return 0.5 * jnp.tanh(0.5 * v) + 0.5


def slot(dr, dc):
    return (dr + 1) * 3 + (dc + 1)


def body(sizes, frames, weight, bias, hid_out, cell_out,
         xc, xe, hc, col_x, col_h, w, ax, ah, acc, cell_mem,
         local_sem, send_sem, xrecv):
    nsec, nrow, ncol = sizes
    steps, rows, cols, width = frames.shape
    pad = steps
    wide = cols + 2 * SIDE
    sec, row, col = lax.axis_index("section"), lax.axis_index("row"), lax.axis_index("col")

    def load_frame(t):
        return pltpu.make_async_copy(frames.at[t], xc.at[t, pl.ds(pad, rows)], local_sem.at[t])

    load_w = pltpu.make_async_copy(weight.at[0], w, local_sem.at[steps])

    @pl.when(sec == 0)
    def _():
        for t in range(steps):
            load_frame(t).start()

    load_w.start()

    def there(dr, dc):
        ok = sec >= 0
        if dr:
            ok = (row > 0) if dr < 0 else (row < nrow - 1)
        if dc:
            okc = (col > 0) if dc < 0 else (col < ncol - 1)
            ok = jnp.logical_and(ok, okc) if dr else okc
        return ok

    def device(ds, dr, dc):
        return {"section": sec + ds, "row": row + dr, "col": col + dc}

    barrier = pltpu.get_barrier_semaphore()

    for t in range(steps):
        xc[t, 0:pad] = jnp.zeros((pad, cols, width), jnp.bfloat16)
        xc[t, pad + rows:] = jnp.zeros((pad, cols, width), jnp.bfloat16)
        xe[t] = jnp.zeros(xe.shape[1:], jnp.bfloat16)

    for ds in (-1, 0, 1):
        okd = (sec > 0) if ds < 0 else (sec < nsec - 1) if ds > 0 else (sec == 0)
        for dr, dc in [(0, 0)] + DIRS:
            if ds == 0 and (dr, dc) == (0, 0):
                continue

            @pl.when(jnp.logical_and(there(dr, dc), okd))
            def _(ds=ds, dr=dr, dc=dc):
                pl.semaphore_signal(barrier, inc=1, device_id=device(ds, dr, dc), device_id_type=MESH)

    def extent(pos, count):
        return 1 + jnp.where(pos > 0, 1, 0) + jnp.where(pos < count - 1, 1, 0)

    near = extent(row, nrow) * extent(col, ncol)
    pl.semaphore_wait(barrier, (extent(sec, nsec) - 1) * near + jnp.where(sec == 0, near - 1, 0))

    def halo_copy(center, base, colbuf, t, kind, ds, dr, dc):
        reach = steps - t
        if dr == 0:
            mine, theirs = pl.ds(0, rows), pl.ds(pad, rows)
        elif dr < 0:
            mine, theirs = pl.ds(0, reach), pl.ds(pad + rows, reach)
        else:
            mine, theirs = pl.ds(rows - reach, reach), pl.ds(pad - reach, reach)
        if dc == 0:
            src = center.at[t, pl.ds(base + (rows - reach if dr > 0 else 0), reach)]
            dst = xc.at[t, theirs]
        else:
            src = colbuf.at[t, 1 if dc > 0 else 0, mine]
            dst = xe.at[t, 0 if dc > 0 else 1, theirs]
        return pltpu.make_async_remote_copy(
            src_ref=src, dst_ref=dst,
            send_sem=send_sem.at[t, kind, slot(dr, dc)],
            recv_sem=xrecv.at[t, slot(-dr, -dc)],
            device_id=device(ds, dr, dc), device_id_type=MESH,
        )

    def halo_sends(act, center, base, colbuf, t, kind, ds):
        for dr, dc in sorted(DIRS, key=lambda d: -abs(d[0]) - abs(d[1])):
            @pl.when(there(dr, dc))
            def _(dr=dr, dc=dc):
                copy = halo_copy(center, base, colbuf, t, kind, ds, dr, dc)
                copy.start() if act == "start" else copy.wait_send()

    def halo_waits(t):
        reach = steps - t
        for dr, dc in DIRS:
            @pl.when(there(dr, dc))
            def _(dr=dr, dc=dc):
                mine = pl.ds(pad, rows) if dr == 0 else pl.ds(pad - reach if dr < 0 else pad + rows, reach)
                dst = xc.at[t, mine] if dc == 0 else xe.at[t, 0 if dc < 0 else 1, mine]
                pltpu.make_async_remote_copy(
                    src_ref=dst, dst_ref=dst,
                    send_sem=send_sem.at[t, 0, slot(0, 0)],
                    recv_sem=xrecv.at[t, slot(dr, dc)],
                    device_id=device(0, dr, dc), device_id_type=MESH,
                ).wait_recv()

    def center_copy(t):
        return pltpu.make_async_remote_copy(
            src_ref=hc.at[t], dst_ref=xc.at[t, pl.ds(pad, rows)],
            send_sem=send_sem.at[t, 0, slot(0, 0)], recv_sem=xrecv.at[t, slot(0, 0)],
            device_id=device(1, 0, 0), device_id_type=MESH,
        )

    @pl.when(sec == 0)
    def _():
        for t in range(steps):
            load_frame(t).wait()
            value = xc[t, pad:pad + rows].astype(jnp.float32)
            col_x[t, 0] = value[:, :SIDE].astype(jnp.bfloat16)
            col_x[t, 1] = value[:, cols - SIDE:].astype(jnp.bfloat16)
            halo_sends("start", xc, pad, col_x, t, 1, 0)

    place = lax.broadcasted_iota(jnp.int32, (wide, width), 0)
    left = jnp.where(col > 0, 1.0, 0.0)
    right = jnp.where(col < ncol - 1, 1.0, 0.0)
    inside = jnp.where(place < SIDE, left, jnp.where(place >= SIDE + cols, right, 1.0))
    above = jnp.where(row > 0, 1.0, 0.0)
    below = jnp.where(row < nrow - 1, 1.0, 0.0)

    def put(out, r, line, full):
        shifted = [pltpu.roll(line, 1, 0), line, pltpu.roll(line, wide - 1, 0)]
        for k, v in enumerate(shifted):
            v = v if full else v[SIDE:SIDE + cols]
            out[r, 0:v.shape[0], k * width:(k + 1) * width] = v.astype(jnp.bfloat16)

    def patches(a, first, count, span):
        return jnp.concatenate(
            [a[first + k:first + k + count, 0:span].reshape(count * span, 3 * width) for k in (-1, 0, 1)], axis=-1
        )

    def kernel_of(half):
        return w[:, half * width:(half + 1) * width, :].reshape(9 * width, 4 * width)

    for t in range(steps):
        e = steps - 1 - t
        full = t < steps - 1
        span = wide if full else cols
        first, last = pad - e, pad + rows + e
        total = (last - first) * span
        if t > 0:
            acc[0:total] = jnp.dot(patches(ah, first, last - first, span), kernel_of(1),
                                   preferred_element_type=jnp.float32)

        @pl.when(sec > 0)
        def _(t=t):
            center = xc.at[t, pl.ds(pad, rows)]
            pltpu.make_async_remote_copy(
                src_ref=center, dst_ref=center, send_sem=send_sem.at[t, 0, slot(0, 0)],
                recv_sem=xrecv.at[t, slot(0, 0)], device_id=device(-1, 0, 0), device_id_type=MESH,
            ).wait_recv()

        halo_waits(t)
        for r in range(first - 1, last + 1):
            line = jnp.concatenate([v.astype(jnp.float32) for v in (xe[t, 0, r], xc[t, r], xe[t, 1, r])], axis=0)
            put(ax, r, line, full)
        if t == 0:
            load_w.wait()
        for r in range(first, last, CHUNK):
            count = min(CHUNK, last - r)
            at = (r - first) * span
            pre = jnp.dot(patches(ax, r, count, span), kernel_of(0), preferred_element_type=jnp.float32)
            pre = pre + bias[...]
            if t > 0:
                pre = pre + acc[at:at + count * span]
            cell = sigmoid(pre[:, :width]) * jnp.tanh(pre[:, 2 * width:3 * width])
            cell = cell.reshape(count, span, width)
            if t > 0:
                old = cell_mem[r:r + count]
                old = old if full else old[:, SIDE:SIDE + cols]
                cell = sigmoid(pre[:, width:2 * width]).reshape(count, span, width) * old + cell
            hidden = sigmoid(pre[:, 3 * width:]).reshape(count, span, width) * jnp.tanh(cell)
            if full:
                cell_mem[r:r + count] = cell
            else:
                cell_out[0, r - pad:r - pad + count] = cell
                hid_out[0, r - pad:r - pad + count] = hidden.astype(jnp.bfloat16)
            for q in range(r, r + count):
                line = hidden[q - r]
                core = line[SIDE:SIDE + cols] if full else line
                if pad <= q < pad + rows:
                    hc[t, q - pad] = core.astype(jnp.bfloat16)
                    col_h[t, 0, q - pad] = core[:SIDE].astype(jnp.bfloat16)
                    col_h[t, 1, q - pad] = core[cols - SIDE:].astype(jnp.bfloat16)
                if full:
                    line = line * inside
                    line = line * above if q < pad else line * below if q >= pad + rows else line
                    put(ah, q, line, t + 1 < steps - 1)

        @pl.when(sec < nsec - 1)
        def _(t=t):
            halo_sends("start", hc, 0, col_h, t, 0, 1)
            center_copy(t).start()

    @pl.when(sec == 0)
    def _():
        for t in range(steps):
            halo_sends("wait", xc, pad, col_x, t, 1, 0)

    @pl.when(sec < nsec - 1)
    def _():
        for t in range(steps):
            center_copy(t).wait_send()
            halo_sends("wait", hc, 0, col_h, t, 0, 1)


def solution(mesh):
    sizes = (mesh.shape["section"], mesh.shape["row"], mesh.shape["col"])

    def step(frames, weight, bias):
        steps, rows, cols, width = frames.shape
        high, wide = rows + 2 * steps, cols + 2 * SIDE
        vmem = pl.BlockSpec(memory_space=pltpu.VMEM)
        hbm = pl.BlockSpec(memory_space=pl.ANY)
        bf16 = jnp.bfloat16
        return pl.pallas_call(
            lambda *refs: body(sizes, *refs),
            out_shape=(
                jax.ShapeDtypeStruct((1, rows, cols, width), bf16),
                jax.ShapeDtypeStruct((1, rows, cols, width), jnp.float32),
            ),
            in_specs=[hbm, hbm, vmem],
            out_specs=(vmem, vmem),
            scratch_shapes=[
                pltpu.VMEM((steps, high, cols, width), bf16),
                pltpu.VMEM((steps, 2, high, SIDE, width), bf16),
                pltpu.VMEM((steps, rows, cols, width), bf16),
                pltpu.VMEM((steps, 2, rows, SIDE, width), bf16),
                pltpu.VMEM((steps, 2, rows, SIDE, width), bf16),
                pltpu.VMEM(weight.shape[1:], bf16),
                pltpu.VMEM((high, wide, 3 * width), bf16),
                pltpu.VMEM((high, wide, 3 * width), bf16),
                pltpu.VMEM((high * wide, 4 * width), jnp.float32),
                pltpu.VMEM((high, wide, width), jnp.float32),
                pltpu.SemaphoreType.DMA((steps + 1,)),
                pltpu.SemaphoreType.DMA((steps, 2, 9)),
                pltpu.SemaphoreType.DMA((steps, 9)),
            ],
            compiler_params=pltpu.CompilerParams(collective_id=0, has_side_effects=True),
        )(frames, weight, bias)

    return jax.shard_map(
        step,
        mesh=mesh,
        in_specs=(P(None, "row", "col", None), P("section", None, None, None), P("section", None)),
        out_specs=(P("section", "row", "col", None), P("section", "row", "col", None)),
        check_vma=False,
    )
```

```python
import jax
import jax.numpy as jnp
from jax import lax
from jax.experimental import pallas as pl
from jax.experimental.pallas import tpu as pltpu
from jax.sharding import PartitionSpec as P

MESH = pl.DeviceIdType.MESH
DIRS = [(dr, dc) for dr in (-1, 0, 1) for dc in (-1, 0, 1) if (dr, dc) != (0, 0)]
SIDE = 8
CHUNK = 6


def sigmoid(v):
    return 0.5 * jnp.tanh(0.5 * v) + 0.5


def slot(dr, dc):
    return (dr + 1) * 3 + (dc + 1)


def body(sizes, frames, weight, bias, kept_out, added_out, gate_out,
         xc, xe, hc, col_x, col_h, w, ax, ah, acc, cell_mem,
         local_sem, send_sem, xrecv):
    nsec, nrow, ncol = sizes
    steps, rows, cols, width = frames.shape
    pad = steps
    wide = cols + 2 * SIDE
    sec, row, col = lax.axis_index("section"), lax.axis_index("row"), lax.axis_index("col")

    def load_frame(t):
        return pltpu.make_async_copy(frames.at[t], xc.at[t, pl.ds(pad, rows)], local_sem.at[t])

    load_w = pltpu.make_async_copy(weight.at[0], w, local_sem.at[steps])

    @pl.when(sec == 0)
    def _():
        for t in range(steps):
            load_frame(t).start()

    load_w.start()

    def there(dr, dc):
        ok = sec >= 0
        if dr:
            ok = (row > 0) if dr < 0 else (row < nrow - 1)
        if dc:
            okc = (col > 0) if dc < 0 else (col < ncol - 1)
            ok = jnp.logical_and(ok, okc) if dr else okc
        return ok

    def device(ds, dr, dc):
        return {"section": sec + ds, "row": row + dr, "col": col + dc}

    barrier = pltpu.get_barrier_semaphore()

    for t in range(steps):
        xc[t, 0:pad] = jnp.zeros((pad, cols, width), jnp.bfloat16)
        xc[t, pad + rows:] = jnp.zeros((pad, cols, width), jnp.bfloat16)
        xe[t] = jnp.zeros(xe.shape[1:], jnp.bfloat16)

    for ds in (-1, 0, 1):
        okd = (sec > 0) if ds < 0 else (sec < nsec - 1) if ds > 0 else (sec == 0)
        for dr, dc in [(0, 0)] + DIRS:
            if ds == 0 and (dr, dc) == (0, 0):
                continue

            @pl.when(jnp.logical_and(there(dr, dc), okd))
            def _(ds=ds, dr=dr, dc=dc):
                pl.semaphore_signal(barrier, inc=1, device_id=device(ds, dr, dc), device_id_type=MESH)

    def extent(pos, count):
        return 1 + jnp.where(pos > 0, 1, 0) + jnp.where(pos < count - 1, 1, 0)

    near = extent(row, nrow) * extent(col, ncol)
    pl.semaphore_wait(barrier, (extent(sec, nsec) - 1) * near + jnp.where(sec == 0, near - 1, 0))

    def halo_copy(center, base, colbuf, t, kind, ds, dr, dc):
        reach = steps - t
        if dr == 0:
            mine, theirs = pl.ds(0, rows), pl.ds(pad, rows)
        elif dr < 0:
            mine, theirs = pl.ds(0, reach), pl.ds(pad + rows, reach)
        else:
            mine, theirs = pl.ds(rows - reach, reach), pl.ds(pad - reach, reach)
        if dc == 0:
            src = center.at[t, pl.ds(base + (rows - reach if dr > 0 else 0), reach)]
            dst = xc.at[t, theirs]
        else:
            src = colbuf.at[t, 1 if dc > 0 else 0, mine]
            dst = xe.at[t, 0 if dc > 0 else 1, theirs]
        return pltpu.make_async_remote_copy(
            src_ref=src, dst_ref=dst,
            send_sem=send_sem.at[t, kind, slot(dr, dc)],
            recv_sem=xrecv.at[t, slot(-dr, -dc)],
            device_id=device(ds, dr, dc), device_id_type=MESH,
        )

    def halo_sends(act, center, base, colbuf, t, kind, ds):
        for dr, dc in sorted(DIRS, key=lambda d: -abs(d[0]) - abs(d[1])):
            @pl.when(there(dr, dc))
            def _(dr=dr, dc=dc):
                copy = halo_copy(center, base, colbuf, t, kind, ds, dr, dc)
                copy.start() if act == "start" else copy.wait_send()

    def halo_waits(t):
        reach = steps - t
        for dr, dc in DIRS:
            @pl.when(there(dr, dc))
            def _(dr=dr, dc=dc):
                mine = pl.ds(pad, rows) if dr == 0 else pl.ds(pad - reach if dr < 0 else pad + rows, reach)
                dst = xc.at[t, mine] if dc == 0 else xe.at[t, 0 if dc < 0 else 1, mine]
                pltpu.make_async_remote_copy(
                    src_ref=dst, dst_ref=dst,
                    send_sem=send_sem.at[t, 0, slot(0, 0)],
                    recv_sem=xrecv.at[t, slot(dr, dc)],
                    device_id=device(0, dr, dc), device_id_type=MESH,
                ).wait_recv()

    def center_copy(t):
        return pltpu.make_async_remote_copy(
            src_ref=hc.at[t], dst_ref=xc.at[t, pl.ds(pad, rows)],
            send_sem=send_sem.at[t, 0, slot(0, 0)], recv_sem=xrecv.at[t, slot(0, 0)],
            device_id=device(1, 0, 0), device_id_type=MESH,
        )

    @pl.when(sec == 0)
    def _():
        for t in range(steps):
            load_frame(t).wait()
            value = xc[t, pad:pad + rows].astype(jnp.float32)
            col_x[t, 0] = value[:, :SIDE].astype(jnp.bfloat16)
            col_x[t, 1] = value[:, cols - SIDE:].astype(jnp.bfloat16)
            halo_sends("start", xc, pad, col_x, t, 1, 0)

    place = lax.broadcasted_iota(jnp.int32, (wide, width), 0)
    left = jnp.where(col > 0, 1.0, 0.0)
    right = jnp.where(col < ncol - 1, 1.0, 0.0)
    inside = jnp.where(place < SIDE, left, jnp.where(place >= SIDE + cols, right, 1.0))
    above = jnp.where(row > 0, 1.0, 0.0)
    below = jnp.where(row < nrow - 1, 1.0, 0.0)

    def put(out, r, line, full):
        shifted = [pltpu.roll(line, 1, 0), line, pltpu.roll(line, wide - 1, 0)]
        for k, v in enumerate(shifted):
            v = v if full else v[SIDE:SIDE + cols]
            out[r, 0:v.shape[0], k * width:(k + 1) * width] = v.astype(jnp.bfloat16)

    def patches(a, first, count, span):
        return jnp.concatenate(
            [a[first + k:first + k + count, 0:span].reshape(count * span, 3 * width) for k in (-1, 0, 1)], axis=-1
        )

    def kernel_of(half):
        return w[:, half * width:(half + 1) * width, :].reshape(9 * width, 4 * width)

    for t in range(steps):
        e = steps - 1 - t
        full = t < steps - 1
        span = wide if full else cols
        first, last = pad - e, pad + rows + e
        total = (last - first) * span
        if t > 0:
            acc[0:total] = jnp.dot(patches(ah, first, last - first, span), kernel_of(1),
                                   preferred_element_type=jnp.float32)

        @pl.when(sec > 0)
        def _(t=t):
            center = xc.at[t, pl.ds(pad, rows)]
            pltpu.make_async_remote_copy(
                src_ref=center, dst_ref=center, send_sem=send_sem.at[t, 0, slot(0, 0)],
                recv_sem=xrecv.at[t, slot(0, 0)], device_id=device(-1, 0, 0), device_id_type=MESH,
            ).wait_recv()

        halo_waits(t)
        for r in range(first - 1, last + 1):
            line = jnp.concatenate([v.astype(jnp.float32) for v in (xe[t, 0, r], xc[t, r], xe[t, 1, r])], axis=0)
            put(ax, r, line, full)
        if t == 0:
            load_w.wait()
        for r in range(first, last, CHUNK):
            count = min(CHUNK, last - r)
            at = (r - first) * span
            pre = jnp.dot(patches(ax, r, count, span), kernel_of(0), preferred_element_type=jnp.float32)
            pre = pre + bias[...]
            if t > 0:
                pre = pre + acc[at:at + count * span]
            added = sigmoid(pre[:, :width]) * jnp.tanh(pre[:, 2 * width:3 * width])
            added = added.reshape(count, span, width)
            cell = added
            if t > 0:
                old = cell_mem[r:r + count]
                old = old if full else old[:, SIDE:SIDE + cols]
                kept = sigmoid(pre[:, width:2 * width]).reshape(count, span, width) * old
                cell = kept + added
            opened = sigmoid(pre[:, 3 * width:]).reshape(count, span, width)
            hidden = opened * jnp.tanh(cell)
            if full:
                cell_mem[r:r + count] = cell
            else:
                kept_out[0, r - pad:r - pad + count] = kept
                added_out[0, r - pad:r - pad + count] = added
                gate_out[0, r - pad:r - pad + count] = opened
            for q in range(r, r + count):
                line = hidden[q - r]
                core = line[SIDE:SIDE + cols] if full else line
                if pad <= q < pad + rows:
                    hc[t, q - pad] = core.astype(jnp.bfloat16)
                    col_h[t, 0, q - pad] = core[:SIDE].astype(jnp.bfloat16)
                    col_h[t, 1, q - pad] = core[cols - SIDE:].astype(jnp.bfloat16)
                if full:
                    line = line * inside
                    line = line * above if q < pad else line * below if q >= pad + rows else line
                    put(ah, q, line, t + 1 < steps - 1)

        @pl.when(sec < nsec - 1)
        def _(t=t):
            halo_sends("start", hc, 0, col_h, t, 0, 1)
            center_copy(t).start()

    @pl.when(sec == 0)
    def _():
        for t in range(steps):
            halo_sends("wait", xc, pad, col_x, t, 1, 0)

    @pl.when(sec < nsec - 1)
    def _():
        for t in range(steps):
            center_copy(t).wait_send()
            halo_sends("wait", hc, 0, col_h, t, 0, 1)


def solution(mesh):
    sizes = (mesh.shape["section"], mesh.shape["row"], mesh.shape["col"])

    def step(frames, weight, bias):
        steps, rows, cols, width = frames.shape
        high, wide = rows + 2 * steps, cols + 2 * SIDE
        vmem = pl.BlockSpec(memory_space=pltpu.VMEM)
        hbm = pl.BlockSpec(memory_space=pl.ANY)
        bf16 = jnp.bfloat16
        kept, added, opened = pl.pallas_call(
            lambda *refs: body(sizes, *refs),
            out_shape=(jax.ShapeDtypeStruct((1, rows, cols, width), jnp.float32),) * 3,
            in_specs=[hbm, hbm, vmem],
            out_specs=(vmem, vmem, vmem),
            scratch_shapes=[
                pltpu.VMEM((steps, high, cols, width), bf16),
                pltpu.VMEM((steps, 2, high, SIDE, width), bf16),
                pltpu.VMEM((steps, rows, cols, width), bf16),
                pltpu.VMEM((steps, 2, rows, SIDE, width), bf16),
                pltpu.VMEM((steps, 2, rows, SIDE, width), bf16),
                pltpu.VMEM(weight.shape[1:], bf16),
                pltpu.VMEM((high, wide, 3 * width), bf16),
                pltpu.VMEM((high, wide, 3 * width), bf16),
                pltpu.VMEM((high * wide, 4 * width), jnp.float32),
                pltpu.VMEM((high, wide, width), jnp.float32),
                pltpu.SemaphoreType.DMA((steps + 1,)),
                pltpu.SemaphoreType.DMA((steps, 2, 9)),
                pltpu.SemaphoreType.DMA((steps, 9)),
            ],
            compiler_params=pltpu.CompilerParams(collective_id=0, has_side_effects=True),
        )(frames, weight, bias)
        cell = kept + added
        return (opened * jnp.tanh(cell)).astype(bf16), cell

    return jax.shard_map(
        step,
        mesh=mesh,
        in_specs=(P(None, "row", "col", None), P("section", None, None, None), P("section", None)),
        out_specs=(P("section", "row", "col", None), P("section", "row", "col", None)),
        check_vma=False,
    )
```
